1024 devices in a mesh: expert: 64 (over z, core), tensor: 16 (over x, y).
Axes of the slice: x: 4, y: 4, z: 32, core: 2. Of those that a mesh axis runs over, the one named last changes fastest.
Arguments:
- tokens: bfloat16 [1536, 4096], P('expert', 'tensor'), may hold values from -6 to 6
- grad_out: bfloat16 [1536, 4096], P('expert', 'tensor'), may hold values from -6 to 6
- routing: int32 [1536, 8], P('expert'), may hold values from 0 to 63, all different within a row; in each aligned block of 24 rows (0 to 23, 24 to 47, ...) at most 6 rows name the same one
- gates: float32 [1536, 8], P('expert'), may hold values from 0.1 to 1
- w_in: bfloat16 [64, 4096, 2, 1536], P('expert', None, None, 'tensor'), may hold values from -0.09375 to 0.09375
- w_out: bfloat16 [64, 1536, 4096], P('expert', 'tensor'), may hold values from -0.15625 to 0.15625
Outputs:
- mixed: bfloat16 [1536, 4096], P('expert', 'tensor')
- grad_tokens: bfloat16 [1536, 4096], P('expert', 'tensor')
- grad_w_out: bfloat16 [64, 1536, 4096], P('expert', 'tensor')
The draws below stay inside these ranges and needn't reach their ends.
Inputs may be any that keep to these rules, and one draw needn't show every extreme that they name: `routing`: each row names 8 different experts. Within each group of 24 tokens (the tokens held by one position of the `expert` axis (one token group)) no expert is named by more than 6 tokens, and some group names some expert exactly 6 times.
All inputs are finite; a program needn't handle non-finite values.
Results may differ from the reference program's by a relative error of at most 0.015.
Values may be sent and summed in bfloat16 or wider, within the bound.
No kernel may reach another device: no remote copies, remote signals or barrier semaphores. Data moves between devices by JAX's collectives and lax.ppermute only.
A program may use at most 32 MiB of HBM per device.

```python
import math
import jax
import jax.numpy as jnp
import numpy as np
from jax import lax

D = 4096
FF = 1536
TOPK = 8
TOK_GRP = 24
EXPERTS = 64
CAP = 6
TOKENS = 1536
N_TENSOR = 16


def block_scale(stream_key, shape, split, smallest, largest):
    level, own = 1.0, jax.random.fold_in(stream_key, 6)
    for dim, parts in split:
        draws = jnp.exp(jax.random.uniform(jax.random.fold_in(own, dim), (parts,), jnp.float32, smallest / len(split), largest / len(split)))
        level = level * jnp.repeat(draws, shape[dim] // parts).reshape([-1 if axis == dim else 1 for axis in range(len(shape))])
    return level


def routed_block(rng, own, number, rows, number_of, top, reach, lean):
    sequence = jax.random.permutation(rng, number_of)
    heavy_load, usual = portions_of(number_of, rows * top, reach, lean, True), portions_of(number_of, rows * top, reach, lean, False)
    places = jnp.arange(number_of)

    def named(tallies, rotation):
        used = int((tallies > 0).sum())
        fixed = max(1, used // 4)
        passed = fixed + (places - fixed + rotation * (used - fixed)) % max(1, number_of - fixed)
        return jnp.zeros((number_of,), jnp.int32).at[sequence[jnp.where(places < fixed, places, passed)]].set(jnp.asarray(tallies, jnp.int32))

    tallies = jnp.where(number % 4 == 0, named(heavy_load, number // 4), named(usual, number - number // 4 - 1))
    mixed = jax.random.permutation(jax.random.fold_in(own, 3), number_of)
    giver, sink = mixed[0:number_of // 2 * 2:2], mixed[1:number_of // 2 * 2:2]
    room = jnp.minimum(tallies[giver] - 1, reach - tallies[sink]) // 2
    room = jnp.where((giver == sequence[0]) | (sink == sequence[0]) | (tallies[sink] == 0), 0, jnp.maximum(room, 0))
    passed = jax.random.randint(jax.random.fold_in(own, 4), (number_of // 2,), 0, 1 << 20) % (room + 1)
    tallies = tallies.at[giver].add(-passed).at[sink].add(passed)
    members = jnp.searchsorted(jnp.cumsum(tallies), jnp.arange(rows * top), side="right").astype(jnp.int32)
    grid = members.reshape(top, rows).T
    grid = grid[jax.random.permutation(jax.random.fold_in(own, 1), rows)]
    rotation = jax.random.randint(jax.random.fold_in(own, 2), (rows, 1), 0, top)
    return jnp.take_along_axis(grid, (jnp.arange(top)[None, :] + rotation) % top, axis=1)


def portions_of(number_of, total, bound, lean, full):
    weights = [(1 << 20) // math.isqrt(grade ** lean) + 1 for grade in range(1, number_of + 1)]
    largest = bound if full else min(bound, max(-(-total // number_of), total * weights[0] // sum(weights)))
    least = 1 if total - largest >= number_of - 1 else 0
    holding, surplus = [largest] + [least] * (number_of - 1), total - largest - least * (number_of - 1)
    while surplus > 0:
        candidates = [i for i in range(1, number_of) if holding[i] < largest] or [i for i in range(1, number_of) if holding[i] < bound]
        pool, left = sum([weights[i] for i in candidates]), surplus
        for i in candidates:
            addition = min(bound - holding[i], max(1, left * weights[i] // pool), surplus)
            holding[i] = holding[i] + addition
            surplus = surplus - addition
    return np.array(holding)


def normal_values(stream_key, extent, width, most, cuts=(), held_as=jnp.bfloat16):
    loudness = block_scale(stream_key, extent, cuts, -0.22, 0.18) if cuts else 1.0
    result = jax.random.normal(stream_key, extent, jnp.float32) * width * loudness
    return jnp.minimum(jnp.maximum(result, -most), most).astype(held_as)


def setup_inputs(seed: int = 0) -> dict:
    keys = jax.random.split(jax.random.key(seed), 7)
    tokens = normal_values(keys[0], (TOKENS, D), 1.0, 6.0, ((0, 64), (1, 16)))
    grad_out = normal_values(keys[1], (TOKENS, D), 1.0, 6.0, ((0, 64), (1, 16)))
    routing_keys = jax.random.split(jax.random.fold_in(keys[2], 1), TOKENS // TOK_GRP)
    routing_turns = jax.random.permutation(jax.random.fold_in(keys[2], 3), TOKENS // TOK_GRP)
    routing = jax.vmap(lambda own, number: routed_block(jax.random.fold_in(keys[2], 2), own, number, TOK_GRP, EXPERTS, TOPK, CAP, 2))(routing_keys, routing_turns).reshape((TOKENS, TOPK))
    gates = jnp.clip(0.1 + 0.9 * jax.random.uniform(keys[3], (TOKENS, TOPK), jnp.float32) ** block_scale(keys[3], (TOKENS, TOPK), ((0, 64),), -0.2, 0.2), 0.1, 1.0)
    w_in = normal_values(keys[4], (EXPERTS, D, 2, FF), D ** -0.5, 0.09375, ((0, 64), (3, 16)))
    w_out = normal_values(keys[5], (EXPERTS, FF, D), FF ** -0.5, 0.15625, ((0, 64), (1, 16)))
    return {"tokens": tokens, "grad_out": grad_out, "routing": routing, "gates": gates, "w_in": w_in, "w_out": w_out}


def reference(tokens, grad_out, routing, gates, w_in, w_out):
    groups = TOKENS // TOK_GRP
    slot_rows = groups * CAP
    hidden = FF // N_TENSOR
    grouped = routing.reshape(groups, TOK_GRP, TOPK)
    is_named = (grouped[..., None] == jnp.arange(EXPERTS, dtype=jnp.int32)).astype(jnp.int32)
    counts = jnp.sum(is_named, axis=2)
    before = jnp.cumsum(counts, axis=1) - counts
    slot_index = jnp.sum(is_named * before[:, :, None, :], axis=3).reshape(-1)
    expert_flat = routing.reshape(-1)
    group_flat = (jnp.arange(TOKENS * TOPK, dtype=jnp.int32) // (TOK_GRP * TOPK)).astype(jnp.int32)
    position = (group_flat * CAP + slot_index).astype(jnp.int32)
    table = jnp.full((EXPERTS, slot_rows), TOKENS * TOPK, jnp.int32)
    table = table.at[expert_flat, position].set(jnp.arange(TOKENS * TOPK, dtype=jnp.int32))
    x_rows = jnp.repeat(tokens, TOPK, axis=0)
    x_rows = jnp.concatenate([x_rows, jnp.zeros((1, D), tokens.dtype)], axis=0)
    scaled = (gates[:, :, None] * grad_out[:, None, :].astype(jnp.float32)).astype(jnp.bfloat16)
    scaled = jnp.concatenate([scaled.reshape(TOKENS * TOPK, D), jnp.zeros((1, D), jnp.bfloat16)], axis=0)

    def one_expert(expert_id):
        picks = table[expert_id]
        x_sel = x_rows[picks]
        dy_sel = scaled[picks]
        w_both = w_in[expert_id].reshape(D, 2 * FF)
        gate_up = jnp.dot(x_sel, w_both, preferred_element_type=jnp.float32)
        gate_proj = gate_up[:, :FF]
        up_proj = gate_up[:, FF:]
        sig_gate = jax.nn.sigmoid(gate_proj)
        activation = (gate_proj * sig_gate * up_proj).astype(jnp.bfloat16)
        act_grad = jnp.dot(dy_sel, w_out[expert_id].T, preferred_element_type=jnp.float32)
        grad_gate = act_grad * up_proj * sig_gate * (1.0 + gate_proj * (1.0 - sig_gate))
        grad_up = act_grad * gate_proj * sig_gate
        grad_both = jnp.concatenate([grad_gate, grad_up], axis=1).astype(jnp.bfloat16)
        act_slices = activation.astype(jnp.float32).reshape(slot_rows, N_TENSOR, hidden)
        down_slices = w_out[expert_id].astype(jnp.float32).reshape(N_TENSOR, hidden, D)
        out_parts = jnp.einsum('rsf,sfd->srd', act_slices, down_slices).astype(jnp.bfloat16)
        expert_out = jnp.sum(out_parts.astype(jnp.float32), axis=0)
        grad_slices = grad_both.astype(jnp.float32).reshape(slot_rows, 2, N_TENSOR, hidden)
        in_slices = w_in[expert_id].astype(jnp.float32).reshape(D, 2, N_TENSOR, hidden)
        in_parts = jnp.einsum('rcsf,dcsf->srd', grad_slices, in_slices).astype(jnp.bfloat16)
        input_grad = jnp.sum(in_parts.astype(jnp.float32), axis=0)
        grad_down = jnp.dot(activation.T, dy_sel, preferred_element_type=jnp.float32).astype(jnp.bfloat16)
        return expert_out, input_grad, grad_down

    expert_outs, input_grads, grad_w_out = lax.map(one_expert, jnp.arange(EXPERTS, dtype=jnp.int32))
    pair_out = expert_outs[expert_flat, position].reshape(TOKENS, TOPK, D)
    pair_in = input_grads[expert_flat, position].reshape(TOKENS, TOPK, D)
    mixed = jnp.sum(gates[:, :, None] * pair_out, axis=1).astype(jnp.bfloat16)
    grad_tokens = jnp.sum(pair_in, axis=1).astype(jnp.bfloat16)
    return mixed, grad_tokens, grad_w_out
```

```python
import functools

import jax
import jax.numpy as jnp
import numpy as np
from jax import lax
from jax.experimental import pallas as pl
from jax.experimental.pallas import tpu as pltpu
from jax.sharding import Mesh
from jax.sharding import PartitionSpec as P


BF = jnp.bfloat16
F32 = jnp.float32
NT = (((1,), (1,)), ((), ()))
NN = (((1,), (0,)), ((), ()))
RING = 4
VMEM_BYTES = 24 * 1024 * 1024
PLANE = ("core", "x", "y")
EXPERT = ("z", "core")
SOURCES = 8

_IDS = np.arange(2 * RING * RING).reshape(2, RING, RING)
A_GROUPS = [[int(i) for i in _IDS[0, :, j]] for j in range(RING)] + [
    [int(i) for i in _IDS[1, j, :]] for j in range(RING)
]
B_GROUPS = [[int(i) for i in _IDS[0, j, :]] for j in range(RING)] + [
    [int(i) for i in _IDS[1, :, j]] for j in range(RING)
]


def b_shift(k):
    return [(g[i], g[(i + k) % RING]) for g in B_GROUPS for i in range(RING)]


def dot(lhs, rhs, dims=NN):
    return lax.dot_general(lhs, rhs, dims, preferred_element_type=F32)


def call(kernel, out_shape, *args, flops=0):
    outs = out_shape if isinstance(out_shape, (list, tuple)) else [out_shape]
    moved = sum(int(np.prod(o.shape)) * o.dtype.itemsize for o in outs)
    moved += sum(int(np.prod(o.shape)) * o.dtype.itemsize for o in args)
    specs = [pl.BlockSpec(memory_space=pltpu.SMEM)]
    specs += [pl.BlockSpec(memory_space=pltpu.VMEM) for _ in args[1:]]
    vmem = pl.BlockSpec(memory_space=pltpu.VMEM)
    single = not isinstance(out_shape, (list, tuple))
    return pl.pallas_call(
        kernel,
        out_shape=out_shape,
        in_specs=specs,
        out_specs=vmem if single else [vmem] * len(out_shape),
        compiler_params=pltpu.CompilerParams(vmem_limit_bytes=VMEM_BYTES),
        cost_estimate=pl.CostEstimate(flops=flops, bytes_accessed=moved, transcendentals=0),
    )(*args)


def shape(*dims, dtype=BF):
    return jax.ShapeDtypeStruct(dims, dtype)


def slice_of(core, a, b):
    return jnp.where(core == 0, a * RING + b, b * RING + a)


def weights_kernel(where, w_in, w_out, *outs):
    hidden, width = w_out.shape
    part = width // (RING * RING)
    core, b = where[0], where[1]
    for k, out in enumerate(outs):
        to = lax.rem(b + k, RING)
        for a in range(RING):
            start = pl.multiple_of(slice_of(core, a, to) * part, part)
            cols = pl.ds(start, part)
            dst = slice(a * part, (a + 1) * part)
            out[0:hidden, dst] = w_in[0, :, cols]
            out[hidden : 2 * hidden, dst] = w_in[1, :, cols]
            out[2 * hidden :, dst] = w_out[:, cols]


def naming(routing, gates, cap, gated):
    tokens, topk = routing.shape
    lane = lax.broadcasted_iota(jnp.int32, (tokens, 128), 1)
    named = jnp.zeros((tokens, 128), F32)
    gate = jnp.zeros((tokens, 128), F32)
    for k in range(topk):
        hit = routing[:, k : k + 1] == lane
        named = jnp.where(hit, 1.0, named)
        gate = jnp.where(hit, gates[:, k : k + 1], gate)
    row = lax.broadcasted_iota(jnp.int32, (tokens, tokens), 0)
    col = lax.broadcasted_iota(jnp.int32, (tokens, tokens), 1)
    before = dot(jnp.where(col < row, 1.0, 0.0).astype(BF), named.astype(BF))
    position = [jnp.where(named > 0.5, before + float(c * cap), -1.0) for c in range(len(gated))]
    factor = [gate if scaled else named for scaled in gated]
    return jnp.concatenate(position, axis=0), jnp.concatenate(factor, axis=0)


def pack_kernel(cap, experts, where, tokens_ref, grad_ref, routing_ref, gates_ref, out):
    del where
    tokens = tokens_ref.shape[0]
    halves = tokens_ref.shape[1] // 128
    slots = out.shape[0] // experts
    gated = (False,) * halves + (True,) * halves
    position, factor = naming(routing_ref[...], gates_ref[...], cap, gated)
    spare = 128 - position.shape[0]
    position = jnp.concatenate([position, jnp.full((spare, 128), -1.0, F32)], axis=0).T
    factor = jnp.concatenate([factor, jnp.zeros((spare, 128), F32)], axis=0).T
    values = [tokens_ref[:, 128 * c : 128 * (c + 1)].astype(F32) for c in range(halves)]
    values += [grad_ref[:, 128 * c : 128 * (c + 1)].astype(F32) for c in range(halves)]
    values = jnp.concatenate(values + [jnp.zeros((spare, 128), F32)], axis=0).astype(BF)
    slot = lax.broadcasted_iota(jnp.int32, (slots, 128), 0).astype(F32)
    picks, scales = [], []
    for e in range(experts):
        pick = position[e : e + 1, :] == slot
        scale = jnp.where(pick, factor[e : e + 1, :], 0.0)
        scales.append(jnp.sum(scale, axis=1, keepdims=True))
        picks.append(jnp.where(pick, 1.0, 0.0))
    rows = dot(jnp.concatenate(picks, axis=0).astype(BF), values)
    out[...] = (rows * jnp.concatenate(scales, axis=0)).astype(BF)


def shuffle(chunks, cap, inverse):
    size = SOURCES * chunks * cap
    line = lax.broadcasted_iota(jnp.int32, (size, size), 1 if inverse else 0)
    other = lax.broadcasted_iota(jnp.int32, (size, size), 0 if inverse else 1)
    chunk = lax.div(line, SOURCES * cap)
    source = lax.div(lax.rem(line, SOURCES * cap), cap)
    wanted = source * (chunks * cap) + chunk * cap + lax.rem(line, cap)
    return jnp.where(other == wanted, 1.0, 0.0).astype(BF)


def arrange_kernel(cap, where, rows_ref, out):
    del where
    chunks = out.shape[2] // 128
    size, part = SOURCES * chunks * cap, SOURCES * cap
    blocks = rows_ref.shape[0] // size
    wide = jnp.concatenate([rows_ref[size * j : size * (j + 1), :] for j in range(blocks)], axis=1)
    wide = dot(shuffle(chunks, cap, False), wide).astype(BF)
    for j in range(blocks):
        for c in range(chunks):
            piece = wide[part * c : part * (c + 1), 128 * j : 128 * (j + 1)]
            for a in range(RING):
                out[a, part * j : part * (j + 1), 128 * c : 128 * (c + 1)] = piece


def total_kernel(cap, where, parts, out):
    del where
    total = parts[0].astype(F32)
    for a in range(1, RING):
        total = total + parts[a].astype(F32)
    total = total.astype(BF)
    chunks = total.shape[1] // 128
    size, part = SOURCES * chunks * cap, SOURCES * cap
    blocks = out.shape[0] // size
    lines = [
        jnp.concatenate(
            [
                total[part * j : part * (j + 1), 128 * c : 128 * (c + 1)]
                for j in range(blocks)
            ],
            axis=1,
        )
        for c in range(chunks)
    ]
    wide = dot(shuffle(chunks, cap, True), jnp.concatenate(lines, axis=0)).astype(BF)
    for j in range(blocks):
        out[size * j : size * (j + 1), :] = wide[:, 128 * j : 128 * (j + 1)]


def home_kernel(cap, experts, where, rows_ref, routing_ref, gates_ref, mixed_ref, grad_ref):
    del where
    tokens = mixed_ref.shape[0]
    halves = mixed_ref.shape[1] // 128
    count = rows_ref.shape[0]
    slots = count // experts
    gated = (True,) * halves + (False,) * halves
    position, factor = naming(routing_ref[...], gates_ref[...], cap, gated)
    row = lax.broadcasted_iota(jnp.int32, (128, count), 0)
    col = lax.broadcasted_iota(jnp.int32, (128, count), 1)
    spread = jnp.where(lax.div(col, slots) == row, 1.0, 0.0)
    slot = lax.rem(lax.broadcasted_iota(jnp.int32, (1, count), 1), slots).astype(F32)
    pick = dot(position.astype(BF), spread.astype(BF)) == slot
    exact = functools.partial(
        lax.dot_general,
        dimension_numbers=NN,
        precision=lax.Precision.HIGHEST,
        preferred_element_type=F32,
    )
    weight = jnp.where(pick, exact(factor, spread), 0.0)
    total = exact(weight, rows_ref[...].astype(F32)).astype(F32)
    for c in range(halves):
        cols = slice(128 * c, 128 * (c + 1))
        mixed_ref[:, cols] = total[tokens * c : tokens * (c + 1)].astype(BF)
        start = tokens * (halves + c)
        grad_ref[:, cols] = total[start : start + tokens].astype(BF)


def up_kernel(where, x_ref, w0, w1, w2, w3, out):
    half = x_ref.shape[2] // 2
    hidden = w0.shape[0] // 3
    x = jnp.concatenate([x_ref[a, :, :half] for a in range(RING)], axis=1)
    dy = jnp.concatenate([x_ref[a, :, half:] for a in range(RING)], axis=1)
    weights = (w0, w1, w2, w3)
    both = jnp.concatenate([w[: 2 * hidden, :] for w in weights], axis=0)
    down = jnp.concatenate([w[2 * hidden :, :] for w in weights], axis=0)
    gate_up = dot(both, x, NT).astype(BF)
    act_grad = dot(down, dy, NT).astype(BF)
    for k in range(RING):
        to = lax.rem(where[1] + (RING - k), RING)
        out[to, : 2 * hidden, :] = gate_up[2 * hidden * k : 2 * hidden * (k + 1)]
        out[to, 2 * hidden :, :] = act_grad[hidden * k : hidden * (k + 1)]


def act_kernel(where, parts, out):
    hidden = parts.shape[1] // 3
    total = parts[0].astype(F32)
    for k in range(1, RING):
        total = total + parts[k].astype(F32)
    gate, up, grad = total[:hidden], total[hidden : 2 * hidden], total[2 * hidden :]
    sig = jax.nn.sigmoid(gate)
    activation = (gate * sig * up).astype(BF)
    grad_gate = (grad * up * sig * (1.0 + gate * (1.0 - sig))).astype(BF)
    grad_up = (grad * gate * sig).astype(BF)
    for k in range(RING):
        out[k, :hidden, :] = activation
        out[k, hidden : 2 * hidden, :] = grad_gate
        out[k, 2 * hidden :, :] = grad_up


def down_kernel(where, h_ref, w0, w1, w2, w3, out):
    hidden = w0.shape[0] // 3
    half = out.shape[2] // 2
    weights = (w0, w1, w2, w3)
    places = [lax.rem(where[1] + (RING - k), RING) for k in range(RING)]
    act_t = jnp.concatenate([h_ref[p, :hidden, :] for p in places], axis=0)
    grad_t = jnp.concatenate([h_ref[p, hidden:, :] for p in places], axis=0)
    down = jnp.concatenate([w[2 * hidden :, :] for w in weights], axis=0)
    both = jnp.concatenate([w[: 2 * hidden, :] for w in weights], axis=0)
    out_part = dot(act_t.T, down).astype(BF)
    in_part = dot(grad_t.T, both).astype(BF)
    for a in range(RING):
        out[a, :, :half] = out_part[:, a * half : (a + 1) * half]
        out[a, :, half:] = in_part[:, a * half : (a + 1) * half]


def grad_kernel(where, h_ref, x_ref, *outs):
    hidden = h_ref.shape[1] // 3
    half = x_ref.shape[2] // 2
    dy = jnp.concatenate([x_ref[a, :, half:] for a in range(RING)], axis=1)
    places = [lax.rem(where[1] + k, RING) for k in range(RING)]
    act_t = jnp.concatenate([h_ref[p, :hidden, :] for p in places], axis=0)
    grad = dot(act_t, dy).astype(BF)
    for k, out in enumerate(outs):
        out[...] = grad[hidden * k : hidden * (k + 1)]


def spread_kernel(where, g0, g1, g2, g3, out):
    part = out.shape[1] // (RING * RING)
    core, b = where[0], where[1]
    for k, g in enumerate((g0, g1, g2, g3)):
        source = lax.rem(b + (RING - k), RING)
        for a in range(RING):
            start = pl.multiple_of(slice_of(core, a, source) * part, part)
            out[:, pl.ds(start, part)] = g[:, a * part : (a + 1) * part]


def exchange(x, axes, groups=None):
    return lax.all_to_all(
        x, axes, split_axis=0, concat_axis=0, tiled=True, axis_index_groups=groups
    )


def shards(tokens, grad_out, routing, gates, w_in, w_out):
    group, part = tokens.shape
    experts = lax.axis_size(EXPERT)
    cap = min(group, 16 * group // experts)
    hidden, width = w_out.shape[1], w_out.shape[2]
    block = width // RING
    slots = cap * (2 * part // 128)
    rows = experts * cap
    core = lax.axis_index("core")
    place_b = jnp.where(core == 0, lax.axis_index("y"), lax.axis_index("x"))
    where = jnp.stack([core, place_b]).astype(jnp.int32)
    fixed = jnp.zeros((2,), jnp.int32)

    sent = call(
        functools.partial(pack_kernel, cap, experts),
        shape(experts * slots, 128),
        fixed,
        tokens,
        grad_out,
        routing,
        gates,
    )
    mine = exchange(sent.reshape(experts, slots, 128), EXPERT)
    w_view = jnp.transpose(w_in[0], (1, 2, 0))
    packed = call(
        weights_kernel, [shape(3 * hidden, block) for _ in range(RING)], where, w_view, w_out[0]
    )
    weights = [packed[0]] + [
        lax.ppermute(packed[k], PLANE, b_shift(k)) for k in range(1, RING)
    ]
    mine, *weights = lax.optimization_barrier((mine, *weights))

    mine = call(
        functools.partial(arrange_kernel, cap),
        shape(RING, rows, 2 * part),
        fixed,
        mine.reshape(experts * slots, 128),
    )
    gathered = exchange(mine, PLANE, A_GROUPS)
    flops = 2 * rows * block * 3 * hidden * RING
    partial = call(up_kernel, shape(RING, 3 * hidden, rows), where, gathered, *weights, flops=flops)
    partial = exchange(partial, PLANE, B_GROUPS)
    units = call(act_kernel, shape(RING, 3 * hidden, rows), where, partial)
    units = exchange(units, PLANE, B_GROUPS)

    back = call(down_kernel, shape(RING, rows, 2 * part), where, units, *weights, flops=flops)
    back = exchange(back, PLANE, A_GROUPS)
    back = call(functools.partial(total_kernel, cap), shape(experts * slots, 128), fixed, back)
    back = exchange(back.reshape(experts, slots, 128), EXPERT)

    grads = call(
        grad_kernel,
        [shape(hidden, block) for _ in range(RING)],
        where,
        units,
        gathered,
        flops=flops // 3,
    )
    grads = [grads[0]] + [lax.ppermute(grads[k], PLANE, b_shift(k)) for k in range(1, RING)]
    grad_down = call(spread_kernel, shape(hidden, width), where, *grads)
    back, grad_down = lax.optimization_barrier((back, grad_down))
    mixed, grad_tokens = call(
        functools.partial(home_kernel, cap, experts),
        [shape(group, part), shape(group, part)],
        fixed,
        back.reshape(experts * slots, 128),
        routing,
        gates,
    )
    return mixed, grad_tokens, grad_down[None]


def solution(mesh):
    experts, _ = mesh.devices.shape
    inner = Mesh(
        mesh.devices.reshape(experts // 2, 2, RING, RING), ("z", "core", "x", "y")
    )
    expert, tensor = EXPERT, ("x", "y")
    in_specs = (
        P(expert, tensor),
        P(expert, tensor),
        P(expert, None),
        P(expert, None),
        P(expert, None, None, tensor),
        P(expert, tensor, None),
    )
    out_specs = (P(expert, tensor), P(expert, tensor), P(expert, tensor, None))
    return jax.shard_map(
        shards, mesh=inner, in_specs=in_specs, out_specs=out_specs, check_vma=False
    )
```

```python
import functools

import jax
import jax.numpy as jnp
import numpy as np
from jax import lax
from jax.experimental import pallas as pl
from jax.experimental.pallas import tpu as pltpu
from jax.sharding import Mesh
from jax.sharding import PartitionSpec as P


BF = jnp.bfloat16
F32 = jnp.float32
NT = (((1,), (1,)), ((), ()))
NN = (((1,), (0,)), ((), ()))
RING = 4
VMEM_BYTES = 24 * 1024 * 1024
PACK_BYTES = 60 * 1024 * 1024
PLANE = ("core", "x", "y")
EXPERT = ("z", "core")
OUT_TURN, HOME_TURN = 32, 32
SOURCES = 8

_IDS = np.arange(2 * RING * RING).reshape(2, RING, RING)
A_GROUPS = [[int(i) for i in _IDS[0, :, j]] for j in range(RING)] + [
    [int(i) for i in _IDS[1, j, :]] for j in range(RING)
]
B_GROUPS = [[int(i) for i in _IDS[0, j, :]] for j in range(RING)] + [
    [int(i) for i in _IDS[1, :, j]] for j in range(RING)
]


def b_shift(k):
    return [(g[i], g[(i + k) % RING]) for g in B_GROUPS for i in range(RING)]


def dot(lhs, rhs, dims=NN):
    return lax.dot_general(lhs, rhs, dims, preferred_element_type=F32)


def call(kernel, out_shape, *args, flops=0, vmem=VMEM_BYTES):
    outs = out_shape if isinstance(out_shape, (list, tuple)) else [out_shape]
    moved = sum(int(np.prod(o.shape)) * o.dtype.itemsize for o in outs)
    moved += sum(int(np.prod(o.shape)) * o.dtype.itemsize for o in args)
    specs = [pl.BlockSpec(memory_space=pltpu.SMEM)]
    specs += [pl.BlockSpec(memory_space=pltpu.VMEM) for _ in args[1:]]
    whole = pl.BlockSpec(memory_space=pltpu.VMEM)
    single = not isinstance(out_shape, (list, tuple))
    return pl.pallas_call(
        kernel,
        out_shape=out_shape,
        in_specs=specs,
        out_specs=whole if single else [whole] * len(out_shape),
        compiler_params=pltpu.CompilerParams(vmem_limit_bytes=vmem),
        cost_estimate=pl.CostEstimate(flops=flops, bytes_accessed=moved, transcendentals=0),
    )(*args)


def shape(*dims, dtype=BF):
    return jax.ShapeDtypeStruct(dims, dtype)


def slice_of(core, a, b):
    return jnp.where(core == 0, a * RING + b, b * RING + a)


def weights_kernel(where, w_in, w_out, *outs):
    hidden, width = w_out.shape
    part = width // (RING * RING)
    core, b = where[0], where[1]
    for k, out in enumerate(outs):
        to = lax.rem(b + k, RING)
        for a in range(RING):
            start = pl.multiple_of(slice_of(core, a, to) * part, part)
            cols = pl.ds(start, part)
            dst = slice(a * part, (a + 1) * part)
            out[0:hidden, dst] = w_in[0, :, cols]
            out[hidden : 2 * hidden, dst] = w_in[1, :, cols]
            out[2 * hidden :, dst] = w_out[:, cols]


def naming(routing, gates, experts, cap, chunks, gated):
    topk, tokens = routing.shape
    row = lax.broadcasted_iota(jnp.int32, (experts, tokens), 0)
    named = jnp.zeros((experts, tokens), F32)
    gate = jnp.zeros((experts, tokens), F32)
    for k in range(topk):
        hit = routing[k : k + 1, :] == row
        named = jnp.where(hit, 1.0, named)
        gate = jnp.where(hit, gates[k : k + 1, :], gate)
    row = lax.broadcasted_iota(jnp.int32, (tokens, tokens), 0)
    col = lax.broadcasted_iota(jnp.int32, (tokens, tokens), 1)
    before = dot(named.astype(BF), jnp.where(row < col, 1.0, 0.0).astype(BF))
    row = lax.broadcasted_iota(jnp.int32, (tokens, 128), 0)
    col = lax.broadcasted_iota(jnp.int32, (tokens, 128), 1)
    chunk = lax.div(col, tokens)
    repeat = jnp.where(jnp.logical_and(col - chunk * tokens == row, chunk < chunks), 1.0, 0.0)
    named = dot(named.astype(BF), repeat.astype(BF))
    before = dot(before.astype(BF), repeat.astype(BF))
    gate = exact(gate, repeat)
    chunk = lax.div(lax.broadcasted_iota(jnp.int32, (experts, 128), 1), tokens)
    position = jnp.where(named > 0.5, before + (chunk * cap).astype(F32), -1.0)
    return position, jnp.where(gated(chunk), gate, named)


def exact(lhs, rhs):
    return lax.dot_general(
        lhs, rhs, NN, precision=lax.Precision.HIGHEST, preferred_element_type=F32
    )


def pack_kernel(cap, turn, where, tokens_ref, grad_ref, routing_ref, gates_ref, out):
    del where
    tokens = tokens_ref.shape[0]
    halves = tokens_ref.shape[1] // 128
    chunks = 2 * halves
    slots = chunks * cap
    experts = out.shape[0] // slots
    position, factor = naming(
        routing_ref[...], gates_ref[...], experts, cap, chunks, lambda chunk: chunk >= halves
    )
    values = [tokens_ref[:, 128 * c : 128 * (c + 1)].astype(F32) for c in range(halves)]
    values += [grad_ref[:, 128 * c : 128 * (c + 1)].astype(F32) for c in range(halves)]
    values.append(jnp.zeros((128 - chunks * tokens, 128), F32))
    values = jnp.concatenate(values, axis=0).astype(BF)
    slot = lax.broadcasted_iota(jnp.int32, (slots, 128), 0).astype(F32)
    picks, scales = [], []
    for i in range(experts):
        e = (i + turn) % experts
        pick = position[e : e + 1, :] == slot
        scale = jnp.where(pick, factor[e : e + 1, :], 0.0)
        scales.append(jnp.sum(scale, axis=1, keepdims=True))
        picks.append(jnp.where(pick, 1.0, 0.0))
    rows = dot(jnp.concatenate(picks, axis=0).astype(BF), values)
    out[...] = (rows * jnp.concatenate(scales, axis=0)).astype(BF)


def shuffle(chunks, cap, inverse):
    size = SOURCES * chunks * cap
    line = lax.broadcasted_iota(jnp.int32, (size, size), 1 if inverse else 0)
    other = lax.broadcasted_iota(jnp.int32, (size, size), 0 if inverse else 1)
    chunk = lax.div(line, SOURCES * cap)
    source = lax.div(lax.rem(line, SOURCES * cap), cap)
    wanted = source * (chunks * cap) + chunk * cap + lax.rem(line, cap)
    return jnp.where(other == wanted, 1.0, 0.0).astype(BF)


def arrange_kernel(cap, where, rows_ref, out):
    del where
    chunks = out.shape[2] // 128
    size, part = SOURCES * chunks * cap, SOURCES * cap
    blocks = rows_ref.shape[0] // size
    wide = jnp.concatenate([rows_ref[size * j : size * (j + 1), :] for j in range(blocks)], axis=1)
    wide = dot(shuffle(chunks, cap, False), wide).astype(BF)
    for j in range(blocks):
        for c in range(chunks):
            piece = wide[part * c : part * (c + 1), 128 * j : 128 * (j + 1)]
            for a in range(RING):
                out[a, part * j : part * (j + 1), 128 * c : 128 * (c + 1)] = piece


def total_kernel(cap, turn, where, parts, out):
    del where
    total = parts[0].astype(F32)
    for a in range(1, RING):
        total = total + parts[a].astype(F32)
    total = total.astype(BF)
    chunks = total.shape[1] // 128
    size, part = SOURCES * chunks * cap, SOURCES * cap
    blocks = out.shape[0] // size
    lines = [
        jnp.concatenate(
            [total[part * j : part * (j + 1), 128 * c : 128 * (c + 1)] for j in range(blocks)],
            axis=1,
        )
        for c in range(chunks)
    ]
    wide = dot(shuffle(chunks, cap, True), jnp.concatenate(lines, axis=0)).astype(BF)
    for j in range(blocks):
        to = (j + turn // SOURCES) % blocks
        out[size * to : size * (to + 1), :] = wide[:, 128 * j : 128 * (j + 1)]


def home_kernel(cap, turn, where, rows_ref, routing_ref, gates_ref, mixed_ref, grad_ref):
    del where
    tokens = mixed_ref.shape[0]
    halves = mixed_ref.shape[1] // 128
    chunks = 2 * halves
    slots = chunks * cap
    count = rows_ref.shape[0]
    experts = count // slots
    position, factor = naming(
        routing_ref[...], gates_ref[...], experts, cap, chunks, lambda chunk: chunk < halves
    )
    blank = jnp.zeros((128 - experts, 128), F32)
    position = jnp.concatenate([position, blank], axis=0).T
    factor = jnp.concatenate([factor, blank], axis=0).T
    row = lax.broadcasted_iota(jnp.int32, (128, count), 0)
    col = lax.broadcasted_iota(jnp.int32, (128, count), 1)
    expert = lax.rem(lax.div(col, slots) + turn, experts)
    spread = jnp.where(expert == row, 1.0, 0.0).astype(BF)
    slot = lax.rem(lax.broadcasted_iota(jnp.int32, (1, count), 1), slots).astype(F32)
    pick = dot(position.astype(BF), spread) == slot
    rows = rows_ref[...]
    total = jnp.zeros((128, 128), F32)
    for _ in range(3):
        piece = factor.astype(BF)
        factor = factor - piece.astype(F32)
        weight = jnp.where(pick, dot(piece, spread), 0.0)
        total = total + dot(weight.astype(BF), rows)
    for c in range(halves):
        cols = slice(128 * c, 128 * (c + 1))
        mixed_ref[:, cols] = total[tokens * c : tokens * (c + 1)].astype(BF)
        start = tokens * (halves + c)
        grad_ref[:, cols] = total[start : start + tokens].astype(BF)


def up_kernel(where, x_ref, w0, w1, w2, w3, out):
    half = x_ref.shape[2] // 2
    hidden = w0.shape[0] // 3
    x = jnp.concatenate([x_ref[a, :, :half] for a in range(RING)], axis=1)
    dy = jnp.concatenate([x_ref[a, :, half:] for a in range(RING)], axis=1)
    weights = (w0, w1, w2, w3)
    both = jnp.concatenate([w[: 2 * hidden, :] for w in weights], axis=0)
    down = jnp.concatenate([w[2 * hidden :, :] for w in weights], axis=0)
    gate_up = dot(both, x, NT).astype(BF)
    act_grad = dot(down, dy, NT).astype(BF)
    for k in range(RING):
        to = lax.rem(where[1] + (RING - k), RING)
        out[to, : 2 * hidden, :] = gate_up[2 * hidden * k : 2 * hidden * (k + 1)]
        out[to, 2 * hidden :, :] = act_grad[hidden * k : hidden * (k + 1)]


def act_kernel(where, parts, out):
    hidden = parts.shape[1] // 3
    total = parts[0].astype(F32)
    for k in range(1, RING):
        total = total + parts[k].astype(F32)
    gate, up, grad = total[:hidden], total[hidden : 2 * hidden], total[2 * hidden :]
    sig = jax.nn.sigmoid(gate)
    activation = (gate * sig * up).astype(BF)
    grad_gate = (grad * up * sig * (1.0 + gate * (1.0 - sig))).astype(BF)
    grad_up = (grad * gate * sig).astype(BF)
    for k in range(RING):
        out[k, :hidden, :] = activation
        out[k, hidden : 2 * hidden, :] = grad_gate
        out[k, 2 * hidden :, :] = grad_up


def down_kernel(where, h_ref, w0, w1, w2, w3, out):
    hidden = w0.shape[0] // 3
    half = out.shape[2] // 2
    weights = (w0, w1, w2, w3)
    places = [lax.rem(where[1] + (RING - k), RING) for k in range(RING)]
    act_t = jnp.concatenate([h_ref[p, :hidden, :] for p in places], axis=0)
    grad_t = jnp.concatenate([h_ref[p, hidden:, :] for p in places], axis=0)
    down = jnp.concatenate([w[2 * hidden :, :] for w in weights], axis=0)
    both = jnp.concatenate([w[: 2 * hidden, :] for w in weights], axis=0)
    out_part = dot(act_t.T, down).astype(BF)
    in_part = dot(grad_t.T, both).astype(BF)
    for a in range(RING):
        out[a, :, :half] = out_part[:, a * half : (a + 1) * half]
        out[a, :, half:] = in_part[:, a * half : (a + 1) * half]


def grad_kernel(where, h_ref, x_ref, *outs):
    hidden = h_ref.shape[1] // 3
    half = x_ref.shape[2] // 2
    dy = jnp.concatenate([x_ref[a, :, half:] for a in range(RING)], axis=1)
    places = [lax.rem(where[1] + k, RING) for k in range(RING)]
    act_t = jnp.concatenate([h_ref[p, :hidden, :] for p in places], axis=0)
    grad = dot(act_t, dy).astype(BF)
    for k, out in enumerate(outs):
        out[...] = grad[hidden * k : hidden * (k + 1)]


def spread_kernel(where, g0, g1, g2, g3, out):
    part = out.shape[1] // (RING * RING)
    core, b = where[0], where[1]
    for k, g in enumerate((g0, g1, g2, g3)):
        source = lax.rem(b + (RING - k), RING)
        for a in range(RING):
            start = pl.multiple_of(slice_of(core, a, source) * part, part)
            out[:, pl.ds(start, part)] = g[:, a * part : (a + 1) * part]


def turned(count, turn):
    return [[(i + turn) % count for i in range(count)]]


def exchange(x, axes, groups=None):
    return lax.all_to_all(
        x, axes, split_axis=0, concat_axis=0, tiled=True, axis_index_groups=groups
    )


def shards(tokens, grad_out, routing, gates, w_in, w_out):
    group, part = tokens.shape
    experts = lax.axis_size(EXPERT)
    cap = min(group, 16 * group // experts)
    hidden, width = w_out.shape[1], w_out.shape[2]
    block = width // RING
    slots = cap * (2 * part // 128)
    rows = experts * cap
    core = lax.axis_index("core")
    place_b = jnp.where(core == 0, lax.axis_index("y"), lax.axis_index("x"))
    where = jnp.stack([core, place_b]).astype(jnp.int32)
    fixed = jnp.zeros((2,), jnp.int32)

    sent = call(
        functools.partial(pack_kernel, cap, OUT_TURN),
        shape(experts * slots, 128),
        fixed,
        tokens,
        grad_out,
        routing.T,
        gates.T,
        vmem=PACK_BYTES,
    )
    mine = exchange(sent.reshape(experts, slots, 128), EXPERT, turned(experts, OUT_TURN))
    w_view = jnp.transpose(w_in[0], (1, 2, 0))
    packed = call(
        weights_kernel, [shape(3 * hidden, block) for _ in range(RING)], where, w_view, w_out[0]
    )
    weights = [packed[0]] + [
        lax.ppermute(packed[k], PLANE, b_shift(k)) for k in range(1, RING)
    ]
    mine, *weights = lax.optimization_barrier((mine, *weights))

    mine = call(
        functools.partial(arrange_kernel, cap),
        shape(RING, rows, 2 * part),
        fixed,
        mine.reshape(experts * slots, 128),
    )
    gathered = exchange(mine, PLANE, A_GROUPS)
    flops = 2 * rows * block * 3 * hidden * RING
    partial = call(up_kernel, shape(RING, 3 * hidden, rows), where, gathered, *weights, flops=flops)
    partial = exchange(partial, PLANE, B_GROUPS)
    units = call(act_kernel, shape(RING, 3 * hidden, rows), where, partial)
    units = exchange(units, PLANE, B_GROUPS)

    back = call(down_kernel, shape(RING, rows, 2 * part), where, units, *weights, flops=flops)
    back = exchange(back, PLANE, A_GROUPS)
    back = call(
        functools.partial(total_kernel, cap, OUT_TURN - HOME_TURN),
        shape(experts * slots, 128),
        fixed,
        back,
    )
    back = exchange(back.reshape(experts, slots, 128), EXPERT, turned(experts, HOME_TURN))

    grads = call(
        grad_kernel,
        [shape(hidden, block) for _ in range(RING)],
        where,
        units,
        gathered,
        flops=flops // 3,
    )
    grads = [grads[0]] + [lax.ppermute(grads[k], PLANE, b_shift(k)) for k in range(1, RING)]
    grad_down = call(spread_kernel, shape(hidden, width), where, *grads)
    back, grad_down = lax.optimization_barrier((back, grad_down))
    mixed, grad_tokens = call(
        functools.partial(home_kernel, cap, HOME_TURN),
        [shape(group, part), shape(group, part)],
        fixed,
        back.reshape(experts * slots, 128),
        routing.T,
        gates.T,
    )
    return mixed, grad_tokens, grad_down[None]


def solution(mesh):
    experts, _ = mesh.devices.shape
    inner = Mesh(
        mesh.devices.reshape(experts // 2, 2, RING, RING), ("z", "core", "x", "y")
    )
    expert, tensor = EXPERT, ("x", "y")
    in_specs = (
        P(expert, tensor),
        P(expert, tensor),
        P(expert, None),
        P(expert, None),
        P(expert, None, None, tensor),
        P(expert, tensor, None),
    )
    out_specs = (P(expert, tensor), P(expert, tensor), P(expert, tensor, None))
    return jax.shard_map(
        shards, mesh=inner, in_specs=in_specs, out_specs=out_specs, check_vma=False
    )
```

```python
import functools

import jax
import jax.numpy as jnp
import numpy as np
from jax import lax
from jax.experimental import pallas as pl
from jax.experimental.pallas import tpu as pltpu
from jax.sharding import Mesh
from jax.sharding import PartitionSpec as P


BF = jnp.bfloat16
F32 = jnp.float32
NT = (((1,), (1,)), ((), ()))
NN = (((1,), (0,)), ((), ()))
RING = 4
VMEM_BYTES = 24 * 1024 * 1024
PACK_BYTES = 60 * 1024 * 1024
PLANE = ("core", "x", "y")
EXPERT = ("z", "core")
OUT_TURN, HOME_TURN = 32, 32
SOURCES = 8

_IDS = np.arange(2 * RING * RING).reshape(2, RING, RING)
A_GROUPS = [[int(i) for i in _IDS[0, :, j]] for j in range(RING)] + [
    [int(i) for i in _IDS[1, j, :]] for j in range(RING)
]
B_GROUPS = [[int(i) for i in _IDS[0, j, :]] for j in range(RING)] + [
    [int(i) for i in _IDS[1, :, j]] for j in range(RING)
]


def b_shift(k):
    return [(g[i], g[(i + k) % RING]) for g in B_GROUPS for i in range(RING)]


def dot(lhs, rhs, dims=NN):
    return lax.dot_general(lhs, rhs, dims, preferred_element_type=F32)


def call(kernel, out_shape, *args, flops=0, vmem=VMEM_BYTES):
    outs = out_shape if isinstance(out_shape, (list, tuple)) else [out_shape]
    moved = sum(int(np.prod(o.shape)) * o.dtype.itemsize for o in outs)
    moved += sum(int(np.prod(o.shape)) * o.dtype.itemsize for o in args)
    whole = pl.BlockSpec(memory_space=pltpu.VMEM)
    specs = [whole for _ in args]
    if args[0].dtype == jnp.int32 and args[0].ndim == 1:
        specs[0] = pl.BlockSpec(memory_space=pltpu.SMEM)
    single = not isinstance(out_shape, (list, tuple))
    return pl.pallas_call(
        kernel,
        out_shape=out_shape,
        in_specs=specs,
        out_specs=whole if single else [whole] * len(out_shape),
        compiler_params=pltpu.CompilerParams(vmem_limit_bytes=vmem),
        cost_estimate=pl.CostEstimate(flops=flops, bytes_accessed=moved, transcendentals=0),
    )(*args)


def shape(*dims, dtype=BF):
    return jax.ShapeDtypeStruct(dims, dtype)


def slice_of(core, a, b):
    return jnp.where(core == 0, a * RING + b, b * RING + a)


def weights_kernel(where, w_in, w_out, *outs):
    hidden, width = w_out.shape
    part = width // (RING * RING)
    core, b = where[0], where[1]
    for k, out in enumerate(outs):
        to = lax.rem(b + k, RING)
        for a in range(RING):
            start = pl.multiple_of(slice_of(core, a, to) * part, part)
            cols = pl.ds(start, part)
            dst = slice(a * part, (a + 1) * part)
            out[0:hidden, dst] = w_in[0, :, cols]
            out[hidden : 2 * hidden, dst] = w_in[1, :, cols]
            out[2 * hidden :, dst] = w_out[:, cols]


def naming(routing, gates, experts, cap, chunks, gated):
    topk, tokens = routing.shape
    row = lax.broadcasted_iota(jnp.int32, (experts, tokens), 0)
    named = jnp.zeros((experts, tokens), F32)
    gate = jnp.zeros((experts, tokens), F32)
    for k in range(topk):
        hit = routing[k : k + 1, :] == row
        named = jnp.where(hit, 1.0, named)
        gate = jnp.where(hit, gates[k : k + 1, :], gate)
    row = lax.broadcasted_iota(jnp.int32, (tokens, tokens), 0)
    col = lax.broadcasted_iota(jnp.int32, (tokens, tokens), 1)
    before = dot(named.astype(BF), jnp.where(row < col, 1.0, 0.0).astype(BF))
    row = lax.broadcasted_iota(jnp.int32, (tokens, 128), 0)
    col = lax.broadcasted_iota(jnp.int32, (tokens, 128), 1)
    chunk = lax.div(col, tokens)
    repeat = jnp.where(jnp.logical_and(col - chunk * tokens == row, chunk < chunks), 1.0, 0.0)
    named = dot(named.astype(BF), repeat.astype(BF))
    before = dot(before.astype(BF), repeat.astype(BF))
    gate = exact(gate, repeat)
    chunk = lax.div(lax.broadcasted_iota(jnp.int32, (experts, 128), 1), tokens)
    position = jnp.where(named > 0.5, before + (chunk * cap).astype(F32), -1.0)
    return position, jnp.where(gated(chunk), gate, named)


def exact(lhs, rhs):
    return lax.dot_general(
        lhs, rhs, NN, precision=lax.Precision.HIGHEST, preferred_element_type=F32
    )


def pack_kernel(cap, turn, tokens_ref, grad_ref, routing_ref, gates_ref, out):
    tokens = tokens_ref.shape[0]
    halves = tokens_ref.shape[1] // 128
    chunks = 2 * halves
    slots = chunks * cap
    experts = out.shape[0] // slots
    position, factor = naming(
        routing_ref[...], gates_ref[...], experts, cap, chunks, lambda chunk: chunk >= halves
    )
    values = [tokens_ref[:, 128 * c : 128 * (c + 1)].astype(F32) for c in range(halves)]
    values += [grad_ref[:, 128 * c : 128 * (c + 1)].astype(F32) for c in range(halves)]
    values.append(jnp.zeros((128 - chunks * tokens, 128), F32))
    values = jnp.concatenate(values, axis=0).astype(BF)
    slot = lax.broadcasted_iota(jnp.int32, (slots, 128), 0).astype(F32)
    picks, scales = [], []
    for i in range(experts):
        e = (i + turn) % experts
        pick = position[e : e + 1, :] == slot
        scale = jnp.where(pick, factor[e : e + 1, :], 0.0)
        scales.append(jnp.sum(scale, axis=1, keepdims=True))
        picks.append(jnp.where(pick, 1.0, 0.0))
    rows = dot(jnp.concatenate(picks, axis=0).astype(BF), values)
    out[...] = (rows * jnp.concatenate(scales, axis=0)).astype(BF)


def shuffle(chunks, cap, inverse):
    size = SOURCES * chunks * cap
    line = lax.broadcasted_iota(jnp.int32, (1, size), 1)
    outer, inner = (chunks, SOURCES) if inverse else (SOURCES, chunks)
    major = lax.div(line, inner * cap)
    rest = line - major * (inner * cap)
    minor = lax.div(rest, cap)
    wanted = (minor * outer + major) * cap + (rest - minor * cap)
    row = lax.broadcasted_iota(jnp.int32, (size, size), 0)
    return jnp.where(row == wanted, 1.0, 0.0).astype(BF)


def arrange_kernel(cap, rows_ref, out):
    chunks = out.shape[2] // 128
    size, part = SOURCES * chunks * cap, SOURCES * cap
    blocks = rows_ref.shape[0] // size
    wide = jnp.concatenate([rows_ref[size * j : size * (j + 1), :] for j in range(blocks)], axis=1)
    wide = dot(shuffle(chunks, cap, False), wide).astype(BF)
    for j in range(blocks):
        for c in range(chunks):
            piece = wide[part * c : part * (c + 1), 128 * j : 128 * (j + 1)]
            for a in range(RING):
                out[a, part * j : part * (j + 1), 128 * c : 128 * (c + 1)] = piece


def total_kernel(cap, turn, parts, out):
    total = parts[0].astype(F32)
    for a in range(1, RING):
        total = total + parts[a].astype(F32)
    total = total.astype(BF)
    chunks = total.shape[1] // 128
    size, part = SOURCES * chunks * cap, SOURCES * cap
    blocks = out.shape[0] // size
    lines = [
        jnp.concatenate(
            [total[part * j : part * (j + 1), 128 * c : 128 * (c + 1)] for j in range(blocks)],
            axis=1,
        )
        for c in range(chunks)
    ]
    wide = dot(shuffle(chunks, cap, True), jnp.concatenate(lines, axis=0)).astype(BF)
    for j in range(blocks):
        to = (j + turn // SOURCES) % blocks
        out[size * to : size * (to + 1), :] = wide[:, 128 * j : 128 * (j + 1)]


def home_kernel(cap, turn, rows_ref, routing_ref, gates_ref, mixed_ref, grad_ref):
    tokens = mixed_ref.shape[0]
    halves = mixed_ref.shape[1] // 128
    chunks = 2 * halves
    slots = chunks * cap
    count = rows_ref.shape[0]
    experts = count // slots
    position, factor = naming(
        routing_ref[...], gates_ref[...], experts, cap, chunks, lambda chunk: chunk < halves
    )
    blank = jnp.zeros((128 - experts, 128), F32)
    position = jnp.concatenate([position, blank], axis=0).T
    factor = jnp.concatenate([factor, blank], axis=0).T
    row = lax.broadcasted_iota(jnp.int32, (128, count), 0)
    col = lax.broadcasted_iota(jnp.int32, (1, count), 1)
    message = lax.div(col, slots)
    expert = message + turn
    expert = jnp.where(expert >= experts, expert - experts, expert)
    spread = jnp.where(expert == row, 1.0, 0.0).astype(BF)
    slot = (col - message * slots).astype(F32)
    pick = dot(position.astype(BF), spread) == slot
    rows = rows_ref[...]
    total = jnp.zeros((128, 128), F32)
    for _ in range(3):
        piece = factor.astype(BF)
        factor = factor - piece.astype(F32)
        weight = jnp.where(pick, dot(piece, spread), 0.0)
        total = total + dot(weight.astype(BF), rows)
    for c in range(halves):
        cols = slice(128 * c, 128 * (c + 1))
        mixed_ref[:, cols] = total[tokens * c : tokens * (c + 1)].astype(BF)
        start = tokens * (halves + c)
        grad_ref[:, cols] = total[start : start + tokens].astype(BF)


def up_kernel(where, x_ref, w0, w1, w2, w3, out):
    half = x_ref.shape[2] // 2
    hidden = w0.shape[0] // 3
    x = jnp.concatenate([x_ref[a, :, :half] for a in range(RING)], axis=1)
    dy = jnp.concatenate([x_ref[a, :, half:] for a in range(RING)], axis=1)
    weights = (w0, w1, w2, w3)
    both = jnp.concatenate([w[: 2 * hidden, :] for w in weights], axis=0)
    down = jnp.concatenate([w[2 * hidden :, :] for w in weights], axis=0)
    gate_up = dot(both, x, NT).astype(BF)
    act_grad = dot(down, dy, NT).astype(BF)
    for k in range(RING):
        to = lax.rem(where[1] + (RING - k), RING)
        out[to, : 2 * hidden, :] = gate_up[2 * hidden * k : 2 * hidden * (k + 1)]
        out[to, 2 * hidden :, :] = act_grad[hidden * k : hidden * (k + 1)]


def act_kernel(where, parts, out):
    hidden = parts.shape[1] // 3
    total = parts[0].astype(F32)
    for k in range(1, RING):
        total = total + parts[k].astype(F32)
    gate, up, grad = total[:hidden], total[hidden : 2 * hidden], total[2 * hidden :]
    sig = jax.nn.sigmoid(gate)
    activation = (gate * sig * up).astype(BF)
    grad_gate = (grad * up * sig * (1.0 + gate * (1.0 - sig))).astype(BF)
    grad_up = (grad * gate * sig).astype(BF)
    for k in range(RING):
        out[k, :hidden, :] = activation
        out[k, hidden : 2 * hidden, :] = grad_gate
        out[k, 2 * hidden :, :] = grad_up


def down_kernel(where, h_ref, w0, w1, w2, w3, out):
    hidden = w0.shape[0] // 3
    half = out.shape[2] // 2
    weights = (w0, w1, w2, w3)
    places = [lax.rem(where[1] + (RING - k), RING) for k in range(RING)]
    act_t = jnp.concatenate([h_ref[p, :hidden, :] for p in places], axis=0)
    grad_t = jnp.concatenate([h_ref[p, hidden:, :] for p in places], axis=0)
    down = jnp.concatenate([w[2 * hidden :, :] for w in weights], axis=0)
    both = jnp.concatenate([w[: 2 * hidden, :] for w in weights], axis=0)
    out_part = dot(act_t.T, down).astype(BF)
    in_part = dot(grad_t.T, both).astype(BF)
    for a in range(RING):
        out[a, :, :half] = out_part[:, a * half : (a + 1) * half]
        out[a, :, half:] = in_part[:, a * half : (a + 1) * half]


def grad_kernel(where, h_ref, x_ref, *outs):
    hidden = h_ref.shape[1] // 3
    half = x_ref.shape[2] // 2
    dy = jnp.concatenate([x_ref[a, :, half:] for a in range(RING)], axis=1)
    places = [lax.rem(where[1] + k, RING) for k in range(RING)]
    act_t = jnp.concatenate([h_ref[p, :hidden, :] for p in places], axis=0)
    grad = dot(act_t, dy).astype(BF)
    for k, out in enumerate(outs):
        out[...] = grad[hidden * k : hidden * (k + 1)]


def spread_kernel(where, g0, g1, g2, g3, out):
    part = out.shape[1] // (RING * RING)
    core, b = where[0], where[1]
    for k, g in enumerate((g0, g1, g2, g3)):
        source = lax.rem(b + (RING - k), RING)
        for a in range(RING):
            start = pl.multiple_of(slice_of(core, a, source) * part, part)
            out[:, pl.ds(start, part)] = g[:, a * part : (a + 1) * part]


def turned(count, turn):
    return [[(i + turn) % count for i in range(count)]]


def exchange(x, axes, groups=None):
    return lax.all_to_all(
        x, axes, split_axis=0, concat_axis=0, tiled=True, axis_index_groups=groups
    )


def shards(tokens, grad_out, routing, gates, w_in, w_out):
    group, part = tokens.shape
    experts = lax.axis_size(EXPERT)
    cap = min(group, 16 * group // experts)
    hidden, width = w_out.shape[1], w_out.shape[2]
    block = width // RING
    slots = cap * (2 * part // 128)
    rows = experts * cap
    core = lax.axis_index("core")
    place_b = jnp.where(core == 0, lax.axis_index("y"), lax.axis_index("x"))
    where = jnp.stack([core, place_b]).astype(jnp.int32)

    sent = call(
        functools.partial(pack_kernel, cap, OUT_TURN),
        shape(experts * slots, 128),
        tokens,
        grad_out,
        routing.T,
        gates.T,
        vmem=PACK_BYTES,
    )
    mine = exchange(sent.reshape(experts, slots, 128), EXPERT, turned(experts, OUT_TURN))
    w_view = jnp.transpose(w_in[0], (1, 2, 0))
    packed = call(
        weights_kernel, [shape(3 * hidden, block) for _ in range(RING)], where, w_view, w_out[0]
    )
    weights = [packed[0]] + [
        lax.ppermute(packed[k], PLANE, b_shift(k)) for k in range(1, RING)
    ]
    mine, *weights = lax.optimization_barrier((mine, *weights))

    mine = call(
        functools.partial(arrange_kernel, cap),
        shape(RING, rows, 2 * part),
        mine.reshape(experts * slots, 128),
    )
    gathered = exchange(mine, PLANE, A_GROUPS)
    flops = 2 * rows * block * 3 * hidden * RING
    partial = call(up_kernel, shape(RING, 3 * hidden, rows), where, gathered, *weights, flops=flops)
    partial = exchange(partial, PLANE, B_GROUPS)
    units = call(act_kernel, shape(RING, 3 * hidden, rows), where, partial)
    units = exchange(units, PLANE, B_GROUPS)

    back = call(down_kernel, shape(RING, rows, 2 * part), where, units, *weights, flops=flops)
    back = exchange(back, PLANE, A_GROUPS)
    back = call(
        functools.partial(total_kernel, cap, OUT_TURN - HOME_TURN),
        shape(experts * slots, 128),
        back,
    )
    back = exchange(back.reshape(experts, slots, 128), EXPERT, turned(experts, HOME_TURN))

    grads = call(
        grad_kernel,
        [shape(hidden, block) for _ in range(RING)],
        where,
        units,
        gathered,
        flops=flops // 3,
    )
    grads = [grads[0]] + [lax.ppermute(grads[k], PLANE, b_shift(k)) for k in range(1, RING)]
    grad_down = call(spread_kernel, shape(hidden, width), where, *grads)
    back, grad_down = lax.optimization_barrier((back, grad_down))
    mixed, grad_tokens = call(
        functools.partial(home_kernel, cap, HOME_TURN),
        [shape(group, part), shape(group, part)],
        back.reshape(experts * slots, 128),
        routing.T,
        gates.T,
    )
    return mixed, grad_tokens, grad_down[None]


def solution(mesh):
    experts, _ = mesh.devices.shape
    inner = Mesh(
        mesh.devices.reshape(experts // 2, 2, RING, RING), ("z", "core", "x", "y")
    )
    expert, tensor = EXPERT, ("x", "y")
    in_specs = (
        P(expert, tensor),
        P(expert, tensor),
        P(expert, None),
        P(expert, None),
        P(expert, None, None, tensor),
        P(expert, tensor, None),
    )
    out_specs = (P(expert, tensor), P(expert, tensor), P(expert, tensor, None))
    return jax.shard_map(
        shards, mesh=inner, in_specs=in_specs, out_specs=out_specs, check_vma=False
    )
```
